32 devices in a mesh: loop: 4 (over y, x), wide: 8 (over z, core).
Axes of the slice: x: 2, y: 2, z: 4, core: 2. Of those that a mesh axis runs over, the one named last changes fastest.
Arguments:
- feats: bfloat16 [8, 1024, 256], P('wide', 'loop'), may hold values from -6 to 6
- w_first: bfloat16 [256, 1024], replicated, may hold values from -0.375 to 0.375
- w_second: bfloat16 [1024, 256], replicated, may hold values from -0.1875 to 0.1875
- cotangent: bfloat16 [8, 1024, 256], P('wide', 'loop'), may hold values from -0.15625 to 0.15625
- block_values: bfloat16 [4, 8, 80, 64, 64], P('loop', 'wide'), may hold values from -0.25 to 0.25
- row_ptr: int32 [4, 8, 17], P('loop', 'wide'), may hold values from 0 to 80, as said below
- col_idx: int32 [4, 8, 80], P('loop', 'wide'), may hold values from 0 to 31
Outputs:
- propagated: bfloat16 [8, 1024, 256], P('wide', 'loop')
- grad_first: float32 [256, 1024], P('wide')
- grad_second: float32 [1024, 256], P('wide')
The draws below stay inside these ranges and needn't reach their ends.
Inputs may be any that keep to these rules, and one draw needn't show every extreme that they name: In each tile row_ptr starts at 0, never falls, and its last entry (the tile's live blocks) is at most 80; in every draw some tile has exactly 80 live blocks. `col_idx`: entries of empty slots are ignored.
All inputs are finite; a program needn't handle non-finite values.
Results may differ from the reference program's by a relative error of at most 0.02.
Values may be sent and summed in bfloat16 or wider, within the bound.
A program may use at most 128 MiB of HBM per device.

```python
import jax
import jax.numpy as jnp
from jax import lax

D = 256
HID = 1024
BLK = 64
BPR = 8
STEPS = 3
ITEMS_DEV = 256
SLOTS = 80
ROWS_W = 1024
ROWBLK = 16
COLBLK = 32
ITEMS = 8192
N_LOOP = 4
N_WIDE = 8


def draw_row_ptr(key, part):
    key_count, key_hot, key_pick, key_rows = jax.random.split(jax.random.fold_in(key, 17), 4)
    tile_total = N_LOOP * N_WIDE
    counts = jax.random.randint(key_count, (tile_total,), SLOTS // 8, SLOTS // 2 + 1)
    heavy = jax.random.randint(key_hot, (tile_total,), 0, 8) == 0
    chosen = jax.random.randint(key_pick, (), 0, tile_total)
    heavy = heavy | (jnp.arange(tile_total) == chosen)
    counts = jnp.where(heavy, SLOTS, counts)
    block_rows = jax.random.randint(key_rows, (tile_total, SLOTS), 0, ROWBLK)
    block_rows = jnp.where(jnp.arange(SLOTS)[None, :] < counts[:, None], block_rows, ROWBLK)
    block_rows = jnp.sort(block_rows, axis=1)
    bounds = jnp.arange(ROWBLK + 1)
    pointers = jnp.sum((block_rows[:, None, :] < bounds[None, :, None]).astype(jnp.int32), axis=2)
    return pointers.reshape(N_LOOP, N_WIDE, ROWBLK + 1).astype(jnp.int32)


def touch_ends(array, stream_key, smallest, high):
    longest = array.shape.index(max(array.shape))
    spots = []
    for shift in (0, 1):
        where = [jax.random.randint(jax.random.fold_in(stream_key, axis), (), 0, length) for axis, length in enumerate(array.shape)]
        where[longest] = (where[longest] + shift) % array.shape[longest]
        spots.append(tuple(where))
    return array.at[spots[0]].set(smallest).at[spots[1]].set(high)


def raised(entries, stream_key, source, target, parts, factor):
    owner, partner = [(jnp.arange(entries.shape[dim]) // (entries.shape[dim] // parts)).reshape([-1 if axis == dim else 1 for axis in range(entries.ndim)]) for dim in (source, target)]
    chosen = jax.random.permutation(stream_key, parts)[partner]
    strong = (owner == chosen) | (owner == (partner + parts // 2) % parts)
    return jnp.where(strong, factor * entries, entries)


def level_of(rng, shape, cuts, least, high):
    level, own = 1.0, jax.random.fold_in(rng, 6)
    for dim, parts in cuts:
        draws = jnp.exp(jax.random.uniform(jax.random.fold_in(own, dim), (parts,), jnp.float32, least / len(cuts), high / len(cuts)))
        level = level * jnp.repeat(draws, shape[dim] // parts).reshape([-1 if axis == dim else 1 for axis in range(len(shape))])
    return level


def bell_draw(key, extent, deviation, bound, shards=(), kind=jnp.bfloat16):
    array = jax.random.normal(key, extent, jnp.float32) * deviation
    if len(shards) > 0:
        array = level_of(key, extent, shards, -0.22, 0.18) * array
    return jnp.clip(array, min=-bound, max=bound).astype(kind)


def noise_with(stream_key, dims, width, limit, cuts, heavy, kind=jnp.bfloat16):
    drawn = width * jax.random.normal(stream_key, dims, jnp.float32)
    if cuts:
        drawn = drawn * level_of(stream_key, dims, cuts, -0.22, 0.18)
    return jnp.clip(raised(drawn, jax.random.fold_in(stream_key, 3), *heavy), -limit, limit).astype(kind)


def setup_inputs(seed: int = 0) -> dict:
    splits = jax.random.split(jax.random.key(seed), 8)
    return {
        "feats": noise_with(splits[0], (N_WIDE, ROWS_W, D), 1.0, 6.0, ((0, 8), (1, 4)), (0, 2, 8, 2.0)),
        "w_first": bell_draw(splits[1], (D, HID), D ** -0.5, 0.375),
        "w_second": bell_draw(splits[2], (HID, D), HID ** -0.5, 0.1875),
        "cotangent": bell_draw(splits[3], (N_WIDE, ROWS_W, D), ((ITEMS_DEV * N_LOOP * N_WIDE) ** -0.5), 0.15625, ((0, 8), (1, 4))),
        "block_values": bell_draw(splits[4], (N_LOOP, N_WIDE, SLOTS, BLK, BLK), (BLK * BPR) ** -0.5, 0.25, ((0, 4), (1, 8))),
        "row_ptr": draw_row_ptr(jax.random.fold_in(splits[7], 71), 0),
        "col_idx": touch_ends(jax.random.randint(splits[6], (N_LOOP, N_WIDE, SLOTS), 0, COLBLK), jax.random.fold_in(splits[6], 1), 0, COLBLK - 1).astype(jnp.int32),
    }


ALPHA = 0.1


def slot_layout(pointers, slot_total):
    slot_ids = jnp.arange(slot_total, dtype=jnp.int32)
    slot_row = jnp.sum((pointers[..., 1:, None] <= slot_ids).astype(jnp.int32), axis=-2)
    slot_live = (slot_ids < pointers[..., -1:]).astype(jnp.float32)
    return jnp.minimum(slot_row, pointers.shape[-1] - 2).astype(jnp.int32), slot_live


def silu_slope(value):
    sigma = jax.nn.sigmoid(value)
    return sigma * (1.0 + value * (1.0 - sigma))


def forward_step(current, teleport, tile_values, slot_row, slot_live, slot_col):
    col_major = current.reshape(N_WIDE, N_LOOP, ITEMS_DEV, D).transpose(1, 0, 2, 3).reshape(N_LOOP, COLBLK, BLK, D)

    def add_loop(summed, pieces):
        col_part, values_part, row_part, live_part, slot_part = pieces
        picked = col_part[slot_part].astype(jnp.float32)
        products = jnp.einsum("wsij,wsjd->wsid", values_part, picked) * live_part[:, :, None, None]
        landed = jax.vmap(lambda prod_one, row_one: jax.ops.segment_sum(prod_one, row_one, num_segments=ROWBLK))(products, row_part)
        return summed + landed, None

    start_sum = jnp.zeros((N_WIDE, ROWBLK, BLK, D), jnp.float32)
    summed, _ = lax.scan(add_loop, start_sum, (col_major, tile_values, slot_row, slot_live, slot_col))
    mixed = (1.0 - ALPHA) * summed.reshape(N_WIDE, ROWS_W, D) + ALPHA * teleport.astype(jnp.float32)
    return mixed.astype(jnp.bfloat16)


def adjoint_step(current, tile_values, slot_row, slot_live, slot_col):
    row_blocks = current.reshape(N_WIDE, ROWBLK, BLK, D)

    def one_loop(pieces):
        values_part, row_part, live_part, slot_part = pieces
        picked = jax.vmap(lambda block_rows, row_one: block_rows[row_one])(row_blocks, row_part).astype(jnp.float32)
        products = jnp.einsum("wsij,wsid->wsjd", values_part, picked) * live_part[:, :, None, None]
        landed = jax.ops.segment_sum(products.reshape(-1, BLK, D), slot_part.reshape(-1), num_segments=COLBLK)
        return landed.reshape(N_WIDE, ITEMS_DEV, D)

    spread = lax.map(one_loop, (tile_values, slot_row, slot_live, slot_col))
    moved = spread.transpose(1, 0, 2, 3).reshape(N_WIDE, ROWS_W, D)
    return ((1.0 - ALPHA) * moved).astype(jnp.bfloat16)


def reference(feats, w_first, w_second, cotangent, block_values, row_ptr, col_idx):
    slot_row, slot_live = slot_layout(row_ptr, SLOTS)
    tile_values = block_values.astype(jnp.float32)
    flat_feats = feats.reshape(ITEMS, D)
    pre_act = jnp.dot(flat_feats, w_first, preferred_element_type=jnp.float32)
    hidden = jax.nn.silu(pre_act).astype(jnp.bfloat16)
    teleport = jnp.dot(hidden, w_second, preferred_element_type=jnp.float32).astype(jnp.bfloat16)
    teleport = teleport.reshape(N_WIDE, ROWS_W, D)
    current = teleport
    for _ in range(STEPS):
        current = forward_step(current, teleport, tile_values, slot_row, slot_live, col_idx)
    adjoint_now = cotangent
    collected = cotangent.astype(jnp.float32)
    for repeat in range(STEPS):
        adjoint_now = adjoint_step(adjoint_now, tile_values, slot_row, slot_live, col_idx)
        if repeat < STEPS - 1:
            collected = collected + adjoint_now.astype(jnp.float32)
    grad_teleport = (ALPHA * collected + adjoint_now.astype(jnp.float32)).astype(jnp.bfloat16).reshape(ITEMS, D)
    grad_hidden = jnp.dot(grad_teleport, w_second.T, preferred_element_type=jnp.float32)
    grad_pre = (grad_hidden * silu_slope(pre_act)).astype(jnp.bfloat16)
    grad_first = jnp.dot(flat_feats.T, grad_pre, preferred_element_type=jnp.float32)
    grad_second = jnp.dot(hidden.T, grad_teleport, preferred_element_type=jnp.float32)
    return current, grad_first, grad_second
```

```python
import functools

import jax
import jax.numpy as jnp
from jax import lax
from jax.experimental import pallas as pl
from jax.experimental.pallas import tpu as pltpu
from jax.sharding import PartitionSpec as P

STEPS = 3


ALPHA = 0.1

MESH = pl.DeviceIdType.MESH


def silu_slope(value):
    sigma = jax.nn.sigmoid(value)
    return sigma * (1.0 + value * (1.0 - sigma))


def dense_kernel(index_ref, core_ref, mine_ref, other_ref, out_ref, acc):
    which, strip = pl.program_id(0), pl.program_id(1)
    chips, rows, cols = out_ref.shape[1], out_ref.shape[3], out_ref.shape[4]
    blk = mine_ref.shape[-1]
    per_strip = rows // blk
    per_chip = cols // (2 * blk)
    upper = lax.broadcasted_iota(jnp.int32, (blk, 2 * blk), 1) // blk
    pointers = index_ref.shape[1] - mine_ref.shape[0]

    def fill(values_ref, tile):
        for row in range(per_strip):
            acc[...] = jnp.zeros_like(acc)
            first = index_ref[tile, strip * per_strip + row]
            last = index_ref[tile, strip * per_strip + row + 1]

            def add(slot, carry):
                col = index_ref[tile, pointers + slot]
                block = values_ref[slot].astype(jnp.float32)
                wide = jnp.concatenate([block, block], axis=1)
                wide = jnp.where(upper == col % 2, wide, 0.0)
                acc[col // 2] = acc[col // 2] + wide
                return carry

            lax.fori_loop(first, last, add, 0)
            for chip in range(chips):
                for part in range(per_chip):
                    out_ref[
                        0, chip, 0, row * blk : (row + 1) * blk, part * 2 * blk : (part + 1) * 2 * blk
                    ] = acc[chip * per_chip + part].astype(out_ref.dtype)

    @pl.when(which == 0)
    def _():
        fill(mine_ref, 0)

    @pl.when(which == 1)
    def _():
        fill(other_ref, 1)


def dense_pair(index, core, mine, other, n_loop, n_chip, items):
    blk = mine.shape[-1]
    cols = 2 * items
    return pl.pallas_call(
        dense_kernel,
        out_shape=jax.ShapeDtypeStruct((n_loop, n_chip, 2, items, cols), jnp.bfloat16),
        grid_spec=pltpu.PrefetchScalarGridSpec(
            num_scalar_prefetch=2,
            grid=(2, n_loop),
            in_specs=[pl.BlockSpec(mine.shape, lambda u, s, idx, core: (0, 0, 0))] * 2,
            out_specs=pl.BlockSpec(
                (1, n_chip, 1, items, cols),
                lambda u, s, idx, core: (s, 0, u + core[0] - 2 * u * core[0], 0, 0),
            ),
            scratch_shapes=[pltpu.VMEM((n_chip * cols // (2 * blk), blk, 2 * blk), jnp.float32)],
        ),
        name="dense_pair",
    )(index, core, mine, other)


def power_kernel(
    n_loop, n_chip, tele_ref, cot_ref, dense_ref, prop_ref, gt_ref,
    tiles, zc, gr, ps, pr, qs, qr, prop_x, gt_x, prop_s, gt_s,
    tile_sem, ex_send, ex_recv, z_send, z_recv, g_send, g_recv, p_send, p_recv, q_send, q_recv,
):
    l = lax.axis_index("loop")
    w = lax.axis_index("wide")
    z, c = w // 2, w % 2
    oc = 1 - c
    items, half = tele_ref.shape[1], tele_ref.shape[2]
    load = pltpu.make_async_copy(dense_ref, tiles, tile_sem)
    load.start()

    barrier = pltpu.get_barrier_semaphore()
    partner = (l, 2 * z + oc)
    chip_peers = [lax.rem(z + j, n_chip) for j in range(1, n_chip)]
    loop_peers = [lax.rem(l + j, n_loop) for j in range(1, n_loop)]
    pl.semaphore_signal(barrier, inc=1, device_id=partner, device_id_type=MESH)
    for zp in chip_peers:
        pl.semaphore_signal(barrier, inc=1, device_id=(l, 2 * zp + c), device_id_type=MESH)
    for lp in loop_peers:
        pl.semaphore_signal(barrier, inc=1, device_id=(lp, w), device_id_type=MESH)
    pl.semaphore_wait(barrier, n_loop + n_chip - 1)

    def remote(src, dst, send, recv, target):
        return pltpu.make_async_remote_copy(
            src_ref=src, dst_ref=dst, send_sem=send, recv_sem=recv,
            device_id=target, device_id_type=MESH,
        )

    def z_copy(k, slot, target):
        return remote(zc.at[k, slot], zc.at[k, slot], z_send.at[k, target], z_recv.at[k, slot], (l, 2 * target + c))

    def g_copy(k, slot, target):
        return remote(gr.at[k, slot], gr.at[k, slot], g_send.at[k, target], g_recv.at[k, slot], (target, w))

    def p_copy(k, slot, target):
        return remote(ps.at[k, target], pr.at[k, slot], p_send.at[k, target], p_recv.at[k, slot], (target, w))

    def q_copy(k, slot, target):
        return remote(qs.at[k, target], qr.at[k, slot], q_send.at[k, target], q_recv.at[k, slot], (l, 2 * target + c))

    cot_x = remote(cot_ref.at[oc], gr.at[0, l, c], ex_send.at[1], ex_recv.at[1], partner)
    cot_x.start()
    tele_x = remote(tele_ref.at[oc], zc.at[0, z, c], ex_send.at[0], ex_recv.at[0], partner)
    tele_x.start()
    gr[0, l, c] = cot_ref[c]
    zc[0, z, c] = tele_ref[c]
    cot_x.wait()
    for lp in loop_peers:
        g_copy(0, l, lp).start()
    tele_x.wait()
    for zp in chip_peers:
        z_copy(0, z, zp).start()
    load.wait()

    def forward_part(k, lp):
        total = None
        for zp in range(n_chip):
            part = jnp.dot(
                tiles[lp, zp].reshape(2 * items, 2 * items),
                zc[k, zp].reshape(2 * items, half),
                preferred_element_type=jnp.float32,
            )
            total = part if total is None else total + part
        return total

    def adjoint_part(k, zp):
        total = None
        for lp in range(n_loop):
            for t in range(2):
                part = jnp.dot(gr[k, lp, t], tiles[lp, zp, t], preferred_element_type=jnp.float32)
                total = part if total is None else total + part
        return total

    for k in range(STEPS):
        for lp in loop_peers:
            g_copy(k, lp, l).wait_recv()

        def q_step(j, carry):
            zp = lax.rem(z + 1 + j, n_chip)
            value = adjoint_part(k, zp).astype(jnp.bfloat16)
            for t in range(2):
                qs[k, zp, t] = value[:, t * items : (t + 1) * items]
            q_copy(k, z, zp).start()
            return carry

        lax.fori_loop(0, n_chip - 1, q_step, 0)
        own_q = adjoint_part(k, z)

        for zp in chip_peers:
            z_copy(k, zp, z).wait_recv()

        def p_step(j, carry):
            lp = lax.rem(l + 1 + j, n_loop)
            ps[k, lp] = forward_part(k, lp).astype(jnp.bfloat16)
            p_copy(k, l, lp).start()
            return carry

        lax.fori_loop(0, n_loop - 1, p_step, 0)
        own_p = forward_part(k, l)

        for zp in chip_peers:
            q_copy(k, zp, z).wait_recv()
        for t in range(2):
            total = own_q[:, t * items : (t + 1) * items]
            for zp in chip_peers:
                total = total + qr[k, zp, t].astype(jnp.float32)
            gr[k + 1, l, t] = ((1.0 - ALPHA) * total).astype(jnp.bfloat16)
        if k < STEPS - 1:
            for lp in loop_peers:
                g_copy(k + 1, l, lp).start()
        else:
            for t in range(2):
                kept = gr[0, l, t].astype(jnp.float32)
                for step in range(1, STEPS):
                    kept = kept + gr[step, l, t].astype(jnp.float32)
                gt_s[t] = (ALPHA * kept + gr[STEPS, l, t].astype(jnp.float32)).astype(jnp.bfloat16)
            gt_copy = remote(gt_s.at[oc], gt_x, ex_send.at[3], ex_recv.at[3], partner)
            gt_copy.start()

        for lp in loop_peers:
            p_copy(k, lp, l).wait_recv()
        total = own_p
        for lp in loop_peers:
            total = total + pr[k, lp].astype(jnp.float32)
        teleport = zc[0, z].reshape(2 * items, half).astype(jnp.float32)
        mixed = ((1.0 - ALPHA) * total + ALPHA * teleport).astype(jnp.bfloat16)
        if k < STEPS - 1:
            for t in range(2):
                zc[k + 1, z, t] = mixed[t * items : (t + 1) * items]
            for zp in chip_peers:
                z_copy(k + 1, z, zp).start()
        else:
            for t in range(2):
                prop_s[t] = mixed[t * items : (t + 1) * items]
            prop_copy = remote(prop_s.at[oc], prop_x, ex_send.at[2], ex_recv.at[2], partner)
            prop_copy.start()

    for k in range(STEPS):
        for zp in chip_peers:
            z_copy(k, z, zp).wait_send()
            q_copy(k, z, zp).wait_send()
        for lp in loop_peers:
            g_copy(k, l, lp).wait_send()
            p_copy(k, l, lp).wait_send()
    gt_copy.wait()
    gt_ref[c] = gt_s[c]
    gt_ref[oc] = gt_x[...]
    prop_copy.wait()
    prop_ref[c] = prop_s[c]
    prop_ref[oc] = prop_x[...]


def power_steps(tele, cot, dense, n_loop, n_chip):
    _, items, half = tele.shape
    bf16, dma = jnp.bfloat16, pltpu.SemaphoreType.DMA
    vmem = pl.BlockSpec(memory_space=pltpu.VMEM)
    return pl.pallas_call(
        functools.partial(power_kernel, n_loop, n_chip),
        out_shape=(
            jax.ShapeDtypeStruct((2, items, half), bf16),
            jax.ShapeDtypeStruct((2, half, items), bf16),
        ),
        in_specs=[vmem, vmem, pl.BlockSpec(memory_space=pl.ANY)],
        out_specs=(vmem, vmem),
        scratch_shapes=[
            pltpu.VMEM(dense.shape, bf16),
            pltpu.VMEM((STEPS, n_chip, 2, items, half), bf16),
            pltpu.VMEM((STEPS + 1, n_loop, 2, half, items), bf16),
            pltpu.VMEM((STEPS, n_loop, 2 * items, half), bf16),
            pltpu.VMEM((STEPS, n_loop, 2 * items, half), bf16),
            pltpu.VMEM((STEPS, n_chip, 2, half, items), bf16),
            pltpu.VMEM((STEPS, n_chip, 2, half, items), bf16),
            pltpu.VMEM((items, half), bf16),
            pltpu.VMEM((half, items), bf16),
            pltpu.VMEM((2, items, half), bf16),
            pltpu.VMEM((2, half, items), bf16),
            dma,
            dma((4,)),
            dma((4,)),
            dma((STEPS, n_chip)),
            dma((STEPS, n_chip)),
            dma((STEPS, n_loop)),
            dma((STEPS, n_loop)),
            dma((STEPS, n_loop)),
            dma((STEPS, n_loop)),
            dma((STEPS, n_chip)),
            dma((STEPS, n_chip)),
        ],
        compiler_params=pltpu.CompilerParams(
            collective_id=0, has_side_effects=True, vmem_limit_bytes=60 * 2**20
        ),
        name="power_steps",
    )(tele, cot, dense)


def body(feats, w_first, w_second, cotangent, block_values, row_ptr, col_idx):
    n_loop, n_wide = lax.axis_size("loop"), lax.axis_size("wide")
    n_chip = n_wide // 2
    mine = block_values[0, 0]
    index = jnp.concatenate([row_ptr[0, 0], col_idx[0, 0]])
    swap = [(i, i + 1 - 2 * (i % 2)) for i in range(n_wide)]
    other = lax.ppermute(mine, "wide", swap)
    other_index = lax.ppermute(index, "wide", swap)
    flat_feats = feats[0]
    items, features = flat_feats.shape
    half = features // 2
    pre_act = jnp.dot(flat_feats, w_first, preferred_element_type=jnp.float32)
    hidden = jax.nn.silu(pre_act).astype(jnp.bfloat16)
    teleport = jnp.dot(hidden, w_second, preferred_element_type=jnp.float32).astype(jnp.bfloat16)
    core = lax.rem(lax.axis_index("wide"), 2).astype(jnp.int32).reshape(1)
    dense = dense_pair(
        jnp.stack([index, other_index]), core, mine, other, n_loop, n_chip, items
    )
    prop_halves, gt_flipped = power_steps(
        teleport.reshape(items, 2, half).transpose(1, 0, 2),
        cotangent[0].T.reshape(2, half, items),
        dense,
        n_loop,
        n_chip,
    )
    current = prop_halves.transpose(1, 0, 2).reshape(items, features)
    grad_teleport = gt_flipped.reshape(features, items).T
    grad_hidden = lax.dot_general(
        grad_teleport, w_second, (((1,), (1,)), ((), ())), preferred_element_type=jnp.float32
    )
    grad_pre = (grad_hidden * silu_slope(pre_act)).astype(jnp.bfloat16)
    contract_items = (((0,), (0,)), ((), ()))
    first_part = lax.psum_scatter(
        lax.dot_general(
            flat_feats, grad_pre, contract_items, preferred_element_type=jnp.float32
        ).astype(jnp.bfloat16),
        "wide",
        scatter_dimension=0,
        tiled=True,
    )
    second_part = lax.psum_scatter(
        lax.dot_general(
            hidden, grad_teleport, contract_items, preferred_element_type=jnp.float32
        ).astype(jnp.bfloat16),
        "wide",
        scatter_dimension=0,
        tiled=True,
    )
    grad_first, grad_second = (
        lax.psum(first_part, "loop").astype(jnp.float32),
        lax.psum(second_part, "loop").astype(jnp.float32),
    )
    return (current[None], grad_first, grad_second)


def solution(mesh):
    return jax.shard_map(
        body,
        mesh=mesh,
        in_specs=(
            P("wide", "loop", None),
            P(),
            P(),
            P("wide", "loop", None),
            P("loop", "wide", None, None, None),
            P("loop", "wide", None),
            P("loop", "wide", None),
        ),
        out_specs=(P("wide", "loop", None), P("wide", None), P("wide", None)),
        check_vma=False,
    )
```

```python
import functools

import jax
import jax.numpy as jnp
from jax import lax
from jax.experimental import pallas as pl
from jax.experimental.pallas import tpu as pltpu
from jax.sharding import PartitionSpec as P

STEPS = 3


ALPHA = 0.1

MESH = pl.DeviceIdType.MESH


def silu_slope(value):
    sigma = jax.nn.sigmoid(value)
    return sigma * (1.0 + value * (1.0 - sigma))


def dense_kernel(index_ref, core_ref, mine_ref, other_ref, out_ref, acc):
    which, strip = pl.program_id(0), pl.program_id(1)
    chips, rows, cols = out_ref.shape[1], out_ref.shape[3], out_ref.shape[4]
    blk = mine_ref.shape[-1]
    per_strip = rows // blk
    per_chip = cols // (2 * blk)
    upper = lax.broadcasted_iota(jnp.int32, (blk, 2 * blk), 1) // blk
    pointers = index_ref.shape[1] - mine_ref.shape[0]

    def fill(values_ref, tile):
        for row in range(per_strip):
            acc[...] = jnp.zeros_like(acc)
            first = index_ref[tile, strip * per_strip + row]
            last = index_ref[tile, strip * per_strip + row + 1]

            def add(slot, carry):
                col = index_ref[tile, pointers + slot]
                block = values_ref[slot].astype(jnp.float32)
                wide = jnp.concatenate([block, block], axis=1)
                wide = jnp.where(upper == col % 2, wide, 0.0)
                acc[col // 2] = acc[col // 2] + wide
                return carry

            lax.fori_loop(first, last, add, 0)
            for chip in range(chips):
                for part in range(per_chip):
                    out_ref[
                        0, chip, 0, row * blk : (row + 1) * blk, part * 2 * blk : (part + 1) * 2 * blk
                    ] = acc[chip * per_chip + part].astype(out_ref.dtype)

    @pl.when(which == 0)
    def _():
        fill(mine_ref, 0)

    @pl.when(which == 1)
    def _():
        fill(other_ref, 1)


def dense_pair(index, core, mine, other, n_loop, n_chip, items):
    blk = mine.shape[-1]
    cols = 2 * items
    return pl.pallas_call(
        dense_kernel,
        out_shape=jax.ShapeDtypeStruct((n_loop, n_chip, 2, items, cols), jnp.bfloat16),
        grid_spec=pltpu.PrefetchScalarGridSpec(
            num_scalar_prefetch=2,
            grid=(2, n_loop),
            in_specs=[pl.BlockSpec(mine.shape, lambda u, s, idx, core: (0, 0, 0))] * 2,
            out_specs=pl.BlockSpec(
                (1, n_chip, 1, items, cols),
                lambda u, s, idx, core: (s, 0, u + core[0] - 2 * u * core[0], 0, 0),
            ),
            scratch_shapes=[pltpu.VMEM((n_chip * cols // (2 * blk), blk, 2 * blk), jnp.float32)],
        ),
        name="dense_pair",
    )(index, core, mine, other)


def power_kernel(
    n_loop, n_chip, tele_ref, cot_ref, feats_ref, hidden_ref, slope_ref, second_ref, dense_ref,
    prop_ref, first_out, second_out,
    tiles, zc, gr, ps, pr, qs, qr, prop_x, gt, prop_s, gt_s,
    f_s, f_x, f_h, f_p, f_q, f_r, f_g, s_s, s_x, s_h, s_p, s_q, s_r, s_g,
    tile_sem, ex_send, ex_recv, z_send, z_recv, g_send, g_recv, p_send, p_recv, q_send, q_recv,
    pair_send, pair_recv, lane_send, lane_recv, chip_send, chip_recv, last_send, last_recv,
):
    l = lax.axis_index("loop")
    w = lax.axis_index("wide")
    z, c = w // 2, w % 2
    oc = 1 - c
    items, half = tele_ref.shape[1], tele_ref.shape[2]
    load = pltpu.make_async_copy(dense_ref, tiles, tile_sem)
    load.start()

    barrier = pltpu.get_barrier_semaphore()
    partner = (l, 2 * z + oc)
    chip_peers = [lax.rem(z + j, n_chip) for j in range(1, n_chip)]
    loop_peers = [lax.rem(l + j, n_loop) for j in range(1, n_loop)]
    pl.semaphore_signal(barrier, inc=1, device_id=partner, device_id_type=MESH)
    for zp in chip_peers:
        pl.semaphore_signal(barrier, inc=1, device_id=(l, 2 * zp + c), device_id_type=MESH)
    for lp in loop_peers:
        pl.semaphore_signal(barrier, inc=1, device_id=(lp, w), device_id_type=MESH)
    pl.semaphore_wait(barrier, n_loop + n_chip - 1)

    def remote(src, dst, send, recv, target):
        return pltpu.make_async_remote_copy(
            src_ref=src, dst_ref=dst, send_sem=send, recv_sem=recv,
            device_id=target, device_id_type=MESH,
        )

    def z_copy(k, slot, target):
        return remote(zc.at[k, slot], zc.at[k, slot], z_send.at[k, target], z_recv.at[k, slot], (l, 2 * target + c))

    def g_copy(k, slot, target):
        return remote(gr.at[k, slot], gr.at[k, slot], g_send.at[k, target], g_recv.at[k, slot], (target, w))

    def p_copy(k, slot, target):
        return remote(ps.at[k, target], pr.at[k, slot], p_send.at[k, target], p_recv.at[k, slot], (target, w))

    def q_copy(k, slot, target):
        return remote(qs.at[k, target], qr.at[k, slot], q_send.at[k, target], q_recv.at[k, slot], (l, 2 * target + c))

    cot_x = remote(cot_ref.at[oc], gr.at[0, l, c], ex_send.at[1], ex_recv.at[1], partner)
    cot_x.start()
    tele_x = remote(tele_ref.at[oc], zc.at[0, z, c], ex_send.at[0], ex_recv.at[0], partner)
    tele_x.start()
    gr[0, l, c] = cot_ref[c]
    zc[0, z, c] = tele_ref[c]
    cot_x.wait()
    for lp in loop_peers:
        g_copy(0, l, lp).start()
    tele_x.wait()
    for zp in chip_peers:
        z_copy(0, z, zp).start()
    load.wait()

    def forward_part(k, lp):
        total = None
        for zp in range(n_chip):
            part = jnp.dot(
                tiles[lp, zp].reshape(2 * items, 2 * items),
                zc[k, zp].reshape(2 * items, half),
                preferred_element_type=jnp.float32,
            )
            total = part if total is None else total + part
        return total

    def adjoint_part(k, zp):
        total = None
        for lp in range(n_loop):
            for t in range(2):
                part = jnp.dot(gr[k, lp, t], tiles[lp, zp, t], preferred_element_type=jnp.float32)
                total = part if total is None else total + part
        return total

    for k in range(STEPS):
        for lp in loop_peers:
            g_copy(k, lp, l).wait_recv()

        def q_step(j, carry):
            zp = lax.rem(z + 1 + j, n_chip)
            value = adjoint_part(k, zp).astype(jnp.bfloat16)
            for t in range(2):
                qs[k, zp, t] = value[:, t * items : (t + 1) * items]
            q_copy(k, z, zp).start()
            return carry

        lax.fori_loop(0, n_chip - 1, q_step, 0)
        own_q = adjoint_part(k, z)

        for zp in chip_peers:
            z_copy(k, zp, z).wait_recv()

        def p_step(j, carry):
            lp = lax.rem(l + 1 + j, n_loop)
            ps[k, lp] = forward_part(k, lp).astype(jnp.bfloat16)
            p_copy(k, l, lp).start()
            return carry

        lax.fori_loop(0, n_loop - 1, p_step, 0)
        own_p = forward_part(k, l)

        for zp in chip_peers:
            q_copy(k, zp, z).wait_recv()
        for t in range(2):
            total = own_q[:, t * items : (t + 1) * items]
            for zp in chip_peers:
                total = total + qr[k, zp, t].astype(jnp.float32)
            gr[k + 1, l, t] = ((1.0 - ALPHA) * total).astype(jnp.bfloat16)
        if k < STEPS - 1:
            for lp in loop_peers:
                g_copy(k + 1, l, lp).start()
        else:
            for t in range(2):
                kept = gr[0, l, t].astype(jnp.float32)
                for step in range(1, STEPS):
                    kept = kept + gr[step, l, t].astype(jnp.float32)
                gt_s[t] = (ALPHA * kept + gr[STEPS, l, t].astype(jnp.float32)).astype(jnp.bfloat16)
            gt_copy = remote(gt_s.at[oc], gt.at[c], ex_send.at[3], ex_recv.at[3], partner)
            gt_copy.start()
            gt[c] = gt_s[c]

        for lp in loop_peers:
            p_copy(k, lp, l).wait_recv()
        total = own_p
        for lp in loop_peers:
            total = total + pr[k, lp].astype(jnp.float32)
        teleport = zc[0, z].reshape(2 * items, half).astype(jnp.float32)
        mixed = ((1.0 - ALPHA) * total + ALPHA * teleport).astype(jnp.bfloat16)
        if k < STEPS - 1:
            for t in range(2):
                zc[k + 1, z, t] = mixed[t * items : (t + 1) * items]
            for zp in chip_peers:
                z_copy(k + 1, z, zp).start()
        else:
            for t in range(2):
                prop_s[t] = mixed[t * items : (t + 1) * items]
            prop_copy = remote(prop_s.at[oc], prop_x, ex_send.at[2], ex_recv.at[2], partner)
            prop_copy.start()

    gt_copy.wait()
    grad_teleport = gt[...].reshape(2 * half, items)
    contract_last = (((1,), (1,)), ((), ()))
    second_sum = lax.dot_general(
        hidden_ref[...], grad_teleport, contract_last, preferred_element_type=jnp.float32
    )
    rows_f, cols_f = f_s.shape[3], f_s.shape[4]
    rows_s = s_s.shape[3]
    for cc in range(2):
        for lp in range(n_loop):
            for zp in range(n_chip):
                row = ((2 * zp + cc) * n_loop + lp) * rows_s
                s_s[cc, lp, zp] = second_sum[row : row + rows_s].astype(jnp.bfloat16)

    def pair_copy(which, src, dst):
        return remote(src.at[oc], dst, pair_send.at[which], pair_recv.at[which], partner)

    def lane_copy(which, src, dst, slot, target):
        return remote(src.at[target], dst.at[slot], lane_send.at[which, target], lane_recv.at[which, slot], (target, w))

    def chip_copy(which, src, dst, slot, target):
        return remote(
            src.at[target], dst.at[slot], chip_send.at[which, target], chip_recv.at[which, slot],
            (l, 2 * target + c),
        )

    def last_copy(which, ref, slot, target):
        return remote(ref.at[slot], ref.at[slot], last_send.at[which, target], last_recv.at[which, slot], (target, w))

    pair_copy(1, s_s, s_x).start()
    grad_hidden = jnp.dot(second_ref[...], grad_teleport, preferred_element_type=jnp.float32)
    grad_pre = (grad_hidden * slope_ref[...]).astype(jnp.bfloat16)
    first_sum = lax.dot_general(
        feats_ref[...], grad_pre, contract_last, preferred_element_type=jnp.float32
    )
    for cc in range(2):
        for lp in range(n_loop):
            for zp in range(n_chip):
                row = (2 * zp + cc) * rows_f
                f_s[cc, lp, zp] = first_sum[
                    row : row + rows_f, lp * cols_f : (lp + 1) * cols_f
                ].astype(jnp.bfloat16)
    pair_copy(0, f_s, f_x).start()
    sets = (
        (1, s_s, s_x, s_h, s_p, s_q, s_r, s_g),
        (0, f_s, f_x, f_h, f_p, f_q, f_r, f_g),
    )
    wide = jnp.float32
    for which, own, got, sums, _p, _q, _r, _g in sets:
        pair_copy(which, own, got).wait()
        for lp in loop_peers:
            sums[lp] = (own[c, lp].astype(wide) + got[lp].astype(wide)).astype(jnp.bfloat16)
            lane_copy(which, sums, _p, l, lp).start()
    for which, own, got, sums, parts, quarter, _r, _g in sets:
        total = own[c, l].astype(wide) + got[l].astype(wide)
        for lp in loop_peers:
            lane_copy(which, sums, parts, lp, l).wait_recv()
            total = total + parts[lp].astype(wide)
        quarter[...] = total.astype(jnp.bfloat16)
        for zp in chip_peers:
            chip_copy(which, quarter, _r, z, zp).start()
    for which, _o, _x, _h, _p, quarter, pieces, final in sets:
        total = quarter[z].astype(wide)
        for zp in chip_peers:
            chip_copy(which, quarter, pieces, zp, z).wait_recv()
            total = total + pieces[zp].astype(wide)
        final[l] = total.astype(jnp.bfloat16)
        for lp in loop_peers:
            last_copy(which, final, l, lp).start()
    prop_copy.wait()
    prop_ref[c] = prop_s[c]
    prop_ref[oc] = prop_x[...]
    for k in range(STEPS):
        for zp in chip_peers:
            z_copy(k, z, zp).wait_send()
            q_copy(k, z, zp).wait_send()
        for lp in loop_peers:
            g_copy(k, l, lp).wait_send()
            p_copy(k, l, lp).wait_send()
    for which, _o, _x, sums, parts, quarter, pieces, final in sets:
        for lp in loop_peers:
            lane_copy(which, sums, parts, l, lp).wait_send()
            last_copy(which, final, l, lp).wait_send()
        for zp in chip_peers:
            chip_copy(which, quarter, pieces, z, zp).wait_send()
        for lp in loop_peers:
            last_copy(which, final, lp, l).wait_recv()
    for lp in range(n_loop):
        first_out[:, lp * cols_f : (lp + 1) * cols_f] = f_g[lp].astype(wide)
        second_out[lp * rows_s : (lp + 1) * rows_s, :] = s_g[lp].astype(wide)


def sum_buffers(n_loop, n_chip, rows, cols):
    shapes = (
        (2, n_loop, n_chip, rows, cols),
        (n_loop, n_chip, rows, cols),
        (n_loop, n_chip, rows, cols),
        (n_loop, n_chip, rows, cols),
        (n_chip, rows, cols),
        (n_chip, rows, cols),
        (n_loop, rows, cols),
    )
    return [pltpu.VMEM(shape, jnp.bfloat16) for shape in shapes]


def power_steps(tele, cot, feats, hidden, slope, second, dense, n_loop, n_chip):
    _, items, half = tele.shape
    features, units = feats.shape[0], hidden.shape[0]
    first_rows, second_rows = features // (2 * n_chip), units // (2 * n_chip)
    bf16, dma = jnp.bfloat16, pltpu.SemaphoreType.DMA
    vmem = pl.BlockSpec(memory_space=pltpu.VMEM)
    return pl.pallas_call(
        functools.partial(power_kernel, n_loop, n_chip),
        out_shape=(
            jax.ShapeDtypeStruct((2, items, half), bf16),
            jax.ShapeDtypeStruct((first_rows, units), jnp.float32),
            jax.ShapeDtypeStruct((second_rows, features), jnp.float32),
        ),
        in_specs=[vmem] * 6 + [pl.BlockSpec(memory_space=pl.ANY)],
        out_specs=(vmem, vmem, vmem),
        scratch_shapes=[
            pltpu.VMEM(dense.shape, bf16),
            pltpu.VMEM((STEPS, n_chip, 2, items, half), bf16),
            pltpu.VMEM((STEPS + 1, n_loop, 2, half, items), bf16),
            pltpu.VMEM((STEPS, n_loop, 2 * items, half), bf16),
            pltpu.VMEM((STEPS, n_loop, 2 * items, half), bf16),
            pltpu.VMEM((STEPS, n_chip, 2, half, items), bf16),
            pltpu.VMEM((STEPS, n_chip, 2, half, items), bf16),
            pltpu.VMEM((items, half), bf16),
            pltpu.VMEM((2, half, items), bf16),
            pltpu.VMEM((2, items, half), bf16),
            pltpu.VMEM((2, half, items), bf16),
            *sum_buffers(n_loop, n_chip, first_rows, units // n_loop),
            *sum_buffers(n_loop, n_chip, second_rows // n_loop, features),
            dma,
            dma((4,)),
            dma((4,)),
            dma((STEPS, n_chip)),
            dma((STEPS, n_chip)),
            dma((STEPS, n_loop)),
            dma((STEPS, n_loop)),
            dma((STEPS, n_loop)),
            dma((STEPS, n_loop)),
            dma((STEPS, n_chip)),
            dma((STEPS, n_chip)),
            dma((2,)),
            dma((2,)),
            dma((2, n_loop)),
            dma((2, n_loop)),
            dma((2, n_chip)),
            dma((2, n_chip)),
            dma((2, n_loop)),
            dma((2, n_loop)),
        ],
        compiler_params=pltpu.CompilerParams(
            collective_id=0, has_side_effects=True, vmem_limit_bytes=63 * 2**20
        ),
        name="power_steps",
    )(tele, cot, feats, hidden, slope, second, dense)


def body(feats, w_first, w_second, cotangent, block_values, row_ptr, col_idx):
    n_loop, n_wide = lax.axis_size("loop"), lax.axis_size("wide")
    n_chip = n_wide // 2
    mine = block_values[0, 0]
    index = jnp.concatenate([row_ptr[0, 0], col_idx[0, 0]])
    swap = [(i, i + 1 - 2 * (i % 2)) for i in range(n_wide)]
    other = lax.ppermute(mine, "wide", swap)
    other_index = lax.ppermute(index, "wide", swap)
    flat_feats = feats[0]
    items, features = flat_feats.shape
    half = features // 2
    pre_act = lax.dot_general(
        w_first, flat_feats, (((0,), (1,)), ((), ())), preferred_element_type=jnp.float32
    )
    hidden = jax.nn.silu(pre_act).astype(jnp.bfloat16)
    teleport = lax.dot_general(
        hidden, w_second, (((0,), (0,)), ((), ())), preferred_element_type=jnp.float32
    ).astype(jnp.bfloat16)
    core = lax.rem(lax.axis_index("wide"), 2).astype(jnp.int32).reshape(1)
    dense = dense_pair(
        jnp.stack([index, other_index]), core, mine, other, n_loop, n_chip, items
    )
    prop_halves, grad_first, grad_second = power_steps(
        teleport.reshape(items, 2, half).transpose(1, 0, 2),
        cotangent[0].T.reshape(2, half, items),
        flat_feats.T,
        hidden,
        silu_slope(pre_act),
        w_second,
        dense,
        n_loop,
        n_chip,
    )
    current = prop_halves.transpose(1, 0, 2).reshape(items, features)
    return (current[None], grad_first, grad_second)


def solution(mesh):
    return jax.shard_map(
        body,
        mesh=mesh,
        in_specs=(
            P("wide", "loop", None),
            P(),
            P(),
            P("wide", "loop", None),
            P("loop", "wide", None, None, None),
            P("loop", "wide", None),
            P("loop", "wide", None),
        ),
        out_specs=(P("wide", "loop", None), P("wide", None), P("wide", None)),
        check_vma=False,
    )
```

```python
import functools

import jax
import jax.numpy as jnp
from jax import lax
from jax.experimental import pallas as pl
from jax.experimental.pallas import tpu as pltpu
from jax.sharding import PartitionSpec as P

STEPS = 3


ALPHA = 0.1

MESH = pl.DeviceIdType.MESH


def silu_slope(value):
    sigma = jax.nn.sigmoid(value)
    return sigma * (1.0 + value * (1.0 - sigma))


def dense_kernel(index_ref, core_ref, mine_ref, other_ref, out_ref, acc):
    which, strip = pl.program_id(0), pl.program_id(1)
    chips, rows, cols = out_ref.shape[1], out_ref.shape[3], out_ref.shape[4]
    blk = mine_ref.shape[-1]
    per_strip = rows // blk
    per_chip = cols // (2 * blk)
    upper = lax.broadcasted_iota(jnp.int32, (blk, 2 * blk), 1) // blk
    pointers = index_ref.shape[1] - mine_ref.shape[0]

    def fill(values_ref, tile):
        for row in range(per_strip):
            acc[...] = jnp.zeros_like(acc)
            first = index_ref[tile, strip * per_strip + row]
            last = index_ref[tile, strip * per_strip + row + 1]

            def add(slot, carry):
                col = index_ref[tile, pointers + slot]
                block = values_ref[slot].astype(jnp.float32)
                wide = jnp.concatenate([block, block], axis=1)
                wide = jnp.where(upper == col % 2, wide, 0.0)
                acc[col // 2] = acc[col // 2] + wide
                return carry

            lax.fori_loop(first, last, add, 0)
            for chip in range(chips):
                for part in range(per_chip):
                    out_ref[
                        0, chip, 0, row * blk : (row + 1) * blk, part * 2 * blk : (part + 1) * 2 * blk
                    ] = acc[chip * per_chip + part].astype(out_ref.dtype)

    @pl.when(which == 0)
    def _():
        fill(mine_ref, 0)

    @pl.when(which == 1)
    def _():
        fill(other_ref, 1)


def dense_pair(index, core, mine, other, n_loop, n_chip, items):
    blk = mine.shape[-1]
    cols = 2 * items
    return pl.pallas_call(
        dense_kernel,
        out_shape=jax.ShapeDtypeStruct((n_loop, n_chip, 2, items, cols), jnp.bfloat16),
        grid_spec=pltpu.PrefetchScalarGridSpec(
            num_scalar_prefetch=2,
            grid=(2, n_loop),
            in_specs=[pl.BlockSpec(mine.shape, lambda u, s, idx, core: (0, 0, 0))] * 2,
            out_specs=pl.BlockSpec(
                (1, n_chip, 1, items, cols),
                lambda u, s, idx, core: (s, 0, u + core[0] - 2 * u * core[0], 0, 0),
            ),
            scratch_shapes=[pltpu.VMEM((n_chip * cols // (2 * blk), blk, 2 * blk), jnp.float32)],
        ),
        name="dense_pair",
    )(index, core, mine, other)


def power_kernel(
    n_loop, n_chip, tele_ref, cot_ref, feats_ref, hidden_ref, slope_ref, second_ref, dense_ref,
    prop_ref, first_out, second_out,
    tiles, zc, gr, ps, pr, qs, qr, own_q, prop_x, gt, prop_s, gt_s,
    f_s, f_x, f_h, f_p, f_q, f_r, f_g, s_s, s_x, s_h, s_p, s_q, s_r, s_g,
    tile_sem, ex_send, ex_recv, z_send, z_recv, g_send, g_recv, p_send, p_recv, q_send, q_recv,
    pair_send, pair_recv, lane_send, lane_recv, chip_send, chip_recv, last_send, last_recv,
):
    l = lax.axis_index("loop")
    w = lax.axis_index("wide")
    z, c = w // 2, w % 2
    oc = 1 - c
    items, half = tele_ref.shape[1], tele_ref.shape[2]
    load = pltpu.make_async_copy(dense_ref, tiles, tile_sem)
    load.start()

    barrier = pltpu.get_barrier_semaphore()
    partner = (l, 2 * z + oc)
    chip_peers = [lax.rem(z + j, n_chip) for j in range(1, n_chip)]
    loop_peers = [lax.rem(l + j, n_loop) for j in range(1, n_loop)]
    pl.semaphore_signal(barrier, inc=1, device_id=partner, device_id_type=MESH)
    for zp in chip_peers:
        pl.semaphore_signal(barrier, inc=1, device_id=(l, 2 * zp + c), device_id_type=MESH)
    for lp in loop_peers:
        pl.semaphore_signal(barrier, inc=1, device_id=(lp, w), device_id_type=MESH)
    pl.semaphore_wait(barrier, n_loop + n_chip - 1)

    def remote(src, dst, send, recv, target):
        return pltpu.make_async_remote_copy(
            src_ref=src, dst_ref=dst, send_sem=send, recv_sem=recv,
            device_id=target, device_id_type=MESH,
        )

    def z_copy(k, slot, t, way):
        target = z + 1 - 2 * way
        return remote(
            zc.at[k, slot, t], zc.at[k, slot, t], z_send.at[k, way, slot, t], z_recv.at[k, slot, t],
            (l, 2 * target + c),
        )

    def z_pass(k, slot, held):
        if not held:
            for t in range(2):
                for way, inside in ((0, z < n_chip - 1), (1, z > 0)):
                    pl.when(inside)(lambda t=t, way=way: z_copy(k, slot, t, way).start())
            return
        left, right = z - held, z + held
        for t in range(2):

            @pl.when(left >= 0)
            def _():
                z_copy(k, left, t, 0).wait_recv()
                pl.when(z < n_chip - 1)(lambda: z_copy(k, left, t, 0).start())

            @pl.when(right < n_chip)
            def _():
                z_copy(k, right, t, 1).wait_recv()
                pl.when(z > 0)(lambda: z_copy(k, right, t, 1).start())

    def z_sent(k):
        for t in range(2):
            for slot in range(n_chip):
                pl.when((z >= slot) & (z < n_chip - 1))(
                    lambda: z_copy(k, slot, t, 0).wait_send()
                )
                pl.when((z <= slot) & (z > 0))(lambda: z_copy(k, slot, t, 1).wait_send())

    def g_copy(k, slot, target):
        return remote(gr.at[k, slot], gr.at[k, slot], g_send.at[k, target], g_recv.at[k, slot], (target, w))

    def p_copy(k, slot, target):
        return remote(ps.at[k, target], pr.at[k, slot], p_send.at[k, target], p_recv.at[k, slot], (target, w))

    def q_copy(k, dest, t, way):
        target = z + 1 - 2 * way
        return remote(
            qs.at[k, dest, t], qr.at[k, way, dest, t], q_send.at[k, dest, t], q_recv.at[k, way, dest, t],
            (l, 2 * target + c),
        )

    def q_add(k, dest, way):
        for t in range(2):
            q_copy(k, dest, t, way).wait_recv()
            total = qs[k, dest, t].astype(jnp.float32) + qr[k, way, dest, t].astype(jnp.float32)
            qs[k, dest, t] = total.astype(jnp.bfloat16)
            q_copy(k, dest, t, way).start()

    def q_stage(k, j):
        up, down = n_chip - 1 - j, j
        upper = z >= n_chip // 2
        goes_down = (z < n_chip - 1) & (z > down)
        pl.when(goes_down & upper)(lambda: q_add(k, down, 1))
        pl.when((z > 0) & (z < up))(lambda: q_add(k, up, 0))
        pl.when(goes_down & (z < n_chip // 2))(lambda: q_add(k, down, 1))

    cot_x = remote(cot_ref.at[oc], gr.at[0, l, c], ex_send.at[1], ex_recv.at[1], partner)
    cot_x.start()
    tele_x = remote(tele_ref.at[oc], zc.at[0, z, c], ex_send.at[0], ex_recv.at[0], partner)
    tele_x.start()
    gr[0, l, c] = cot_ref[c]
    zc[0, z, c] = tele_ref[c]
    cot_x.wait()
    for lp in loop_peers:
        g_copy(0, l, lp).start()
    tele_x.wait()
    z_pass(0, z, 0)
    load.wait()

    def forward_part(k, lp):
        total = None
        for zp in range(n_chip):
            part = jnp.dot(
                tiles[lp, zp].reshape(2 * items, 2 * items),
                zc[k, zp].reshape(2 * items, half),
                preferred_element_type=jnp.float32,
            )
            total = part if total is None else total + part
        return total

    def adjoint_part(k, zp):
        total = None
        for lp in range(n_loop):
            for t in range(2):
                part = jnp.dot(gr[k, lp, t], tiles[lp, zp, t], preferred_element_type=jnp.float32)
                total = part if total is None else total + part
        return total

    for k in range(STEPS):
        if n_chip > 1:
            z_pass(k, z, 1)
        for lp in loop_peers:
            g_copy(k, lp, l).wait_recv()

        def q_step(j, carry):
            flip = (2 * z) // n_chip
            zp = (1 - flip) * (n_chip - 1 - j) + flip * j

            @pl.when(zp != z)
            def _():
                value = adjoint_part(k, zp).astype(jnp.bfloat16)
                for t in range(2):
                    qs[k, zp, t] = value[:, t * items : (t + 1) * items]
                for t in range(2):
                    pl.when(z == 0)(lambda: q_copy(k, zp, t, 0).start())
                    pl.when(z == n_chip - 1)(lambda: q_copy(k, zp, t, 1).start())

            return carry

        lax.fori_loop(0, n_chip, q_step, 0)
        own_q[...] = adjoint_part(k, z)
        for held in range(2, n_chip - 1):
            z_pass(k, z, held)
        q_stage(k, 0)
        if n_chip > 2:
            z_pass(k, z, n_chip - 1)

        def p_step(j, carry):
            lp = lax.rem(l + 1 + j, n_loop)
            ps[k, lp] = forward_part(k, lp).astype(jnp.bfloat16)
            p_copy(k, l, lp).start()
            return carry

        lax.fori_loop(0, n_loop - 1, p_step, 0)
        own_p = forward_part(k, l)

        for j in range(1, n_chip - 1):
            q_stage(k, j)
        for t in range(2):
            lanes = slice(t * items, (t + 1) * items)
            for way, inside in ((0, z > 0), (1, z < n_chip - 1)):

                @pl.when(inside)
                def _():
                    q_copy(k, z, t, way).wait_recv()
                    own_q[:, lanes] = own_q[:, lanes] + qr[k, way, z, t].astype(jnp.float32)

            gr[k + 1, l, t] = ((1.0 - ALPHA) * own_q[:, lanes]).astype(jnp.bfloat16)
        if k < STEPS - 1:
            for lp in loop_peers:
                g_copy(k + 1, l, lp).start()
        else:
            for t in range(2):
                kept = gr[0, l, t].astype(jnp.float32)
                for step in range(1, STEPS):
                    kept = kept + gr[step, l, t].astype(jnp.float32)
                gt_s[t] = (ALPHA * kept + gr[STEPS, l, t].astype(jnp.float32)).astype(jnp.bfloat16)
            gt_copy = remote(gt_s.at[oc], gt.at[c], ex_send.at[3], ex_recv.at[3], partner)
            gt_copy.start()
            gt[c] = gt_s[c]

        for lp in loop_peers:
            p_copy(k, lp, l).wait_recv()
        total = own_p
        for lp in loop_peers:
            total = total + pr[k, lp].astype(jnp.float32)
        teleport = zc[0, z].reshape(2 * items, half).astype(jnp.float32)
        mixed = ((1.0 - ALPHA) * total + ALPHA * teleport).astype(jnp.bfloat16)
        if k < STEPS - 1:
            for t in range(2):
                zc[k + 1, z, t] = mixed[t * items : (t + 1) * items]
            z_pass(k + 1, z, 0)
        else:
            for t in range(2):
                prop_s[t] = mixed[t * items : (t + 1) * items]
            prop_copy = remote(prop_s.at[oc], prop_x, ex_send.at[2], ex_recv.at[2], partner)
            prop_copy.start()

    gt_copy.wait()
    grad_teleport = gt[...].reshape(2 * half, items)
    contract_last = (((1,), (1,)), ((), ()))
    second_sum = lax.dot_general(
        hidden_ref[...], grad_teleport, contract_last, preferred_element_type=jnp.float32
    )
    rows_f, cols_f = f_s.shape[3], f_s.shape[4]
    rows_s = s_s.shape[3]
    for cc in range(2):
        for lp in range(n_loop):
            for zp in range(n_chip):
                row = ((2 * zp + cc) * n_loop + lp) * rows_s
                s_s[cc, lp, zp] = second_sum[row : row + rows_s].astype(jnp.bfloat16)

    def pair_copy(which, src, dst):
        return remote(src.at[oc], dst, pair_send.at[which], pair_recv.at[which], partner)

    def lane_copy(which, src, dst, slot, target):
        return remote(src.at[target], dst.at[slot], lane_send.at[which, target], lane_recv.at[which, slot], (target, w))

    def chip_copy(which, src, dst, slot, target):
        return remote(
            src.at[target], dst.at[slot], chip_send.at[which, target], chip_recv.at[which, slot],
            (l, 2 * target + c),
        )

    def last_copy(which, ref, slot, target):
        return remote(ref.at[slot], ref.at[slot], last_send.at[which, target], last_recv.at[which, slot], (target, w))

    pair_copy(1, s_s, s_x).start()
    grad_hidden = jnp.dot(second_ref[...], grad_teleport, preferred_element_type=jnp.float32)
    grad_pre = (grad_hidden * slope_ref[...]).astype(jnp.bfloat16)
    first_sum = lax.dot_general(
        feats_ref[...], grad_pre, contract_last, preferred_element_type=jnp.float32
    )
    for cc in range(2):
        for lp in range(n_loop):
            for zp in range(n_chip):
                row = (2 * zp + cc) * rows_f
                f_s[cc, lp, zp] = first_sum[
                    row : row + rows_f, lp * cols_f : (lp + 1) * cols_f
                ].astype(jnp.bfloat16)
    pair_copy(0, f_s, f_x).start()
    sets = (
        (1, s_s, s_x, s_h, s_p, s_q, s_r, s_g),
        (0, f_s, f_x, f_h, f_p, f_q, f_r, f_g),
    )
    wide = jnp.float32
    for which, own, got, sums, _p, _q, _r, _g in sets:
        pair_copy(which, own, got).wait()
        for lp in loop_peers:
            sums[lp] = (own[c, lp].astype(wide) + got[lp].astype(wide)).astype(jnp.bfloat16)
            lane_copy(which, sums, _p, l, lp).start()
    for which, own, got, sums, parts, quarter, _r, _g in sets:
        total = own[c, l].astype(wide) + got[l].astype(wide)
        for lp in loop_peers:
            lane_copy(which, sums, parts, lp, l).wait_recv()
            total = total + parts[lp].astype(wide)
        quarter[...] = total.astype(jnp.bfloat16)
        for zp in chip_peers:
            chip_copy(which, quarter, _r, z, zp).start()
    for which, _o, _x, _h, _p, quarter, pieces, final in sets:
        total = quarter[z].astype(wide)
        for zp in chip_peers:
            chip_copy(which, quarter, pieces, zp, z).wait_recv()
            total = total + pieces[zp].astype(wide)
        final[l] = total.astype(jnp.bfloat16)
        for lp in loop_peers:
            last_copy(which, final, l, lp).start()
    prop_copy.wait()
    prop_ref[c] = prop_s[c]
    prop_ref[oc] = prop_x[...]
    for k in range(STEPS):
        z_sent(k)
        for t in range(2):
            for dest in range(n_chip):
                pl.when(z < dest)(lambda: q_copy(k, dest, t, 0).wait_send())
                pl.when(z > dest)(lambda: q_copy(k, dest, t, 1).wait_send())
        for lp in loop_peers:
            g_copy(k, l, lp).wait_send()
            p_copy(k, l, lp).wait_send()
    for which, _o, _x, sums, parts, quarter, pieces, final in sets:
        for lp in loop_peers:
            lane_copy(which, sums, parts, l, lp).wait_send()
            last_copy(which, final, l, lp).wait_send()
        for zp in chip_peers:
            chip_copy(which, quarter, pieces, z, zp).wait_send()
        for lp in loop_peers:
            last_copy(which, final, lp, l).wait_recv()
    for lp in range(n_loop):
        first_out[:, lp * cols_f : (lp + 1) * cols_f] = f_g[lp].astype(wide)
        second_out[lp * rows_s : (lp + 1) * rows_s, :] = s_g[lp].astype(wide)


def sum_buffers(n_loop, n_chip, rows, cols):
    shapes = (
        (2, n_loop, n_chip, rows, cols),
        (n_loop, n_chip, rows, cols),
        (n_loop, n_chip, rows, cols),
        (n_loop, n_chip, rows, cols),
        (n_chip, rows, cols),
        (n_chip, rows, cols),
        (n_loop, rows, cols),
    )
    return [pltpu.VMEM(shape, jnp.bfloat16) for shape in shapes]


def power_steps(tele, cot, feats, hidden, slope, second, dense, n_loop, n_chip):
    _, items, half = tele.shape
    features, units = feats.shape[0], hidden.shape[0]
    first_rows, second_rows = features // (2 * n_chip), units // (2 * n_chip)
    bf16, dma = jnp.bfloat16, pltpu.SemaphoreType.DMA
    vmem = pl.BlockSpec(memory_space=pltpu.VMEM)
    return pl.pallas_call(
        functools.partial(power_kernel, n_loop, n_chip),
        out_shape=(
            jax.ShapeDtypeStruct((2, items, half), bf16),
            jax.ShapeDtypeStruct((first_rows, units), jnp.float32),
            jax.ShapeDtypeStruct((second_rows, features), jnp.float32),
        ),
        in_specs=[vmem] * 6 + [pl.BlockSpec(memory_space=pl.ANY)],
        out_specs=(vmem, vmem, vmem),
        scratch_shapes=[
            pltpu.VMEM(dense.shape, bf16),
            pltpu.VMEM((STEPS, n_chip, 2, items, half), bf16),
            pltpu.VMEM((STEPS + 1, n_loop, 2, half, items), bf16),
            pltpu.VMEM((STEPS, n_loop, 2 * items, half), bf16),
            pltpu.VMEM((STEPS, n_loop, 2 * items, half), bf16),
            pltpu.VMEM((STEPS, n_chip, 2, half, items), bf16),
            pltpu.VMEM((STEPS, 2, n_chip, 2, half, items), bf16),
            pltpu.VMEM((half, 2 * items), jnp.float32),
            pltpu.VMEM((items, half), bf16),
            pltpu.VMEM((2, half, items), bf16),
            pltpu.VMEM((2, items, half), bf16),
            pltpu.VMEM((2, half, items), bf16),
            *sum_buffers(n_loop, n_chip, first_rows, units // n_loop),
            *sum_buffers(n_loop, n_chip, second_rows // n_loop, features),
            dma,
            dma((4,)),
            dma((4,)),
            dma((STEPS, 2, n_chip, 2)),
            dma((STEPS, n_chip, 2)),
            dma((STEPS, n_loop)),
            dma((STEPS, n_loop)),
            dma((STEPS, n_loop)),
            dma((STEPS, n_loop)),
            dma((STEPS, n_chip, 2)),
            dma((STEPS, 2, n_chip, 2)),
            dma((2,)),
            dma((2,)),
            dma((2, n_loop)),
            dma((2, n_loop)),
            dma((2, n_chip)),
            dma((2, n_chip)),
            dma((2, n_loop)),
            dma((2, n_loop)),
        ],
        compiler_params=pltpu.CompilerParams(
            collective_id=0, has_side_effects=True, vmem_limit_bytes=63 * 2**20
        ),
        name="power_steps",
    )(tele, cot, feats, hidden, slope, second, dense)


def body(feats, w_first, w_second, cotangent, block_values, row_ptr, col_idx):
    n_loop, n_wide = lax.axis_size("loop"), lax.axis_size("wide")
    n_chip = n_wide // 2
    mine = block_values[0, 0]
    index = jnp.concatenate([row_ptr[0, 0], col_idx[0, 0]])
    swap = [(i, i + 1 - 2 * (i % 2)) for i in range(n_wide)]
    other = lax.ppermute(mine, "wide", swap)
    other_index = lax.ppermute(index, "wide", swap)
    flat_feats = feats[0]
    items, features = flat_feats.shape
    half = features // 2
    pre_act = lax.dot_general(
        w_first, flat_feats, (((0,), (1,)), ((), ())), preferred_element_type=jnp.float32
    )
    hidden = jax.nn.silu(pre_act).astype(jnp.bfloat16)
    teleport = lax.dot_general(
        hidden, w_second, (((0,), (0,)), ((), ())), preferred_element_type=jnp.float32
    ).astype(jnp.bfloat16)
    core = lax.rem(lax.axis_index("wide"), 2).astype(jnp.int32).reshape(1)
    dense = dense_pair(
        jnp.stack([index, other_index]), core, mine, other, n_loop, n_chip, items
    )
    prop_halves, grad_first, grad_second = power_steps(
        teleport.reshape(items, 2, half).transpose(1, 0, 2),
        cotangent[0].T.reshape(2, half, items),
        flat_feats.T,
        hidden,
        silu_slope(pre_act),
        w_second,
        dense,
        n_loop,
        n_chip,
    )
    current = prop_halves.transpose(1, 0, 2).reshape(items, features)
    return (current[None], grad_first, grad_second)


def solution(mesh):
    return jax.shard_map(
        body,
        mesh=mesh,
        in_specs=(
            P("wide", "loop", None),
            P(),
            P(),
            P("wide", "loop", None),
            P("loop", "wide", None, None, None),
            P("loop", "wide", None),
            P("loop", "wide", None),
        ),
        out_specs=(P("wide", "loop", None), P("wide", None), P("wide", None)),
        check_vma=False,
    )
```

```python
import functools

import jax
import jax.numpy as jnp
from jax import lax
from jax.experimental import pallas as pl
from jax.experimental.pallas import tpu as pltpu
from jax.sharding import PartitionSpec as P

STEPS = 3


ALPHA = 0.1

MESH = pl.DeviceIdType.MESH


def silu_slope(value):
    sigma = jax.nn.sigmoid(value)
    return sigma * (1.0 + value * (1.0 - sigma))


def dense_kernel(index_ref, core_ref, mine_ref, other_ref, out_ref, acc):
    which, strip = pl.program_id(0), pl.program_id(1)
    chips, rows, cols = out_ref.shape[1], out_ref.shape[3], out_ref.shape[4]
    blk = mine_ref.shape[-1]
    per_strip = rows // blk
    per_chip = cols // (2 * blk)
    upper = lax.broadcasted_iota(jnp.int32, (blk, 2 * blk), 1) // blk
    pointers = index_ref.shape[1] - mine_ref.shape[0]

    def fill(values_ref, tile):
        for row in range(per_strip):
            acc[...] = jnp.zeros_like(acc)
            first = index_ref[tile, strip * per_strip + row]
            last = index_ref[tile, strip * per_strip + row + 1]

            def add(pair, carry):
                slot = first + 2 * pair
                after = jnp.minimum(slot + 1, last - 1)
                cols = (index_ref[tile, pointers + slot], index_ref[tile, pointers + after])
                sides = (cols[0] % 2, jnp.where(slot + 1 < last, cols[1] % 2, 2))
                blocks = (values_ref[slot].astype(jnp.float32), values_ref[after].astype(jnp.float32))
                wides = [
                    jnp.where(upper == side, jnp.concatenate([block, block], axis=1), 0.0)
                    for side, block in zip(sides, blocks)
                ]
                for col, wide in zip(cols, wides):
                    acc[col // 2] = acc[col // 2] + wide
                return carry

            lax.fori_loop(0, (last - first + 1) // 2, add, 0)
            for chip in range(chips):
                for part in range(per_chip):
                    out_ref[
                        0, chip, 0, row * blk : (row + 1) * blk, part * 2 * blk : (part + 1) * 2 * blk
                    ] = acc[chip * per_chip + part].astype(out_ref.dtype)

    @pl.when(which == 0)
    def _():
        fill(mine_ref, 0)

    @pl.when(which == 1)
    def _():
        fill(other_ref, 1)


def dense_pair(index, core, mine, other, n_loop, n_chip, items):
    blk = mine.shape[-1]
    cols = 2 * items
    return pl.pallas_call(
        dense_kernel,
        out_shape=jax.ShapeDtypeStruct((n_loop, n_chip, 2, items, cols), jnp.bfloat16),
        grid_spec=pltpu.PrefetchScalarGridSpec(
            num_scalar_prefetch=2,
            grid=(2, n_loop),
            in_specs=[pl.BlockSpec(mine.shape, lambda u, s, idx, core: (0, 0, 0))] * 2,
            out_specs=pl.BlockSpec(
                (1, n_chip, 1, items, cols),
                lambda u, s, idx, core: (s, 0, u + core[0] - 2 * u * core[0], 0, 0),
            ),
            scratch_shapes=[pltpu.VMEM((n_chip * cols // (2 * blk), blk, 2 * blk), jnp.float32)],
        ),
        name="dense_pair",
    )(index, core, mine, other)


def power_kernel(
    n_loop, n_chip, tele_ref, cot_ref, feats_ref, hidden_ref, slope_ref, second_ref, dense_ref,
    prop_ref, first_out, second_out,
    tiles, zc, gr, ps, pr, qs, qr, own_q, prop_x, gt, prop_s, gt_s,
    f_s, f_x, f_h, f_p, f_q, f_r, f_g, s_s, s_x, s_h, s_p, s_q, s_r, s_g,
    tile_sem, ex_send, ex_recv, z_send, z_recv, g_send, g_recv, p_send, p_recv, q_send, q_recv,
    pair_send, pair_recv, lane_send, lane_recv, chip_send, chip_recv, last_send, last_recv,
):
    l = lax.axis_index("loop")
    w = lax.axis_index("wide")
    z, c = w // 2, w % 2
    oc = 1 - c
    items, half = tele_ref.shape[1], tele_ref.shape[2]
    load = pltpu.make_async_copy(dense_ref, tiles, tile_sem)
    load.start()

    barrier = pltpu.get_barrier_semaphore()
    partner = (l, 2 * z + oc)
    chip_peers = [lax.rem(z + j, n_chip) for j in range(1, n_chip)]
    loop_peers = [lax.rem(l + j, n_loop) for j in range(1, n_loop)]
    pl.semaphore_signal(barrier, inc=1, device_id=partner, device_id_type=MESH)
    for zp in chip_peers:
        pl.semaphore_signal(barrier, inc=1, device_id=(l, 2 * zp + c), device_id_type=MESH)
    for lp in loop_peers:
        pl.semaphore_signal(barrier, inc=1, device_id=(lp, w), device_id_type=MESH)
    pl.semaphore_wait(barrier, n_loop + n_chip - 1)

    def remote(src, dst, send, recv, target):
        return pltpu.make_async_remote_copy(
            src_ref=src, dst_ref=dst, send_sem=send, recv_sem=recv,
            device_id=target, device_id_type=MESH,
        )

    def z_copy(k, slot, t, way):
        target = z + 1 - 2 * way
        return remote(
            zc.at[k, slot, t], zc.at[k, slot, t], z_send.at[k, way, slot, t], z_recv.at[k, slot, t],
            (l, 2 * target + c),
        )

    def z_pass(k, slot, held):
        if not held:
            for t in range(2):
                for way, inside in ((0, z < n_chip - 1), (1, z > 0)):
                    pl.when(inside)(lambda t=t, way=way: z_copy(k, slot, t, way).start())
            return
        left, right = z - held, z + held
        for t in range(2):

            @pl.when(left >= 0)
            def _():
                z_copy(k, left, t, 0).wait_recv()
                pl.when(z < n_chip - 1)(lambda: z_copy(k, left, t, 0).start())

            @pl.when(right < n_chip)
            def _():
                z_copy(k, right, t, 1).wait_recv()
                pl.when(z > 0)(lambda: z_copy(k, right, t, 1).start())

    def z_sent(k):
        for t in range(2):
            for slot in range(n_chip):
                pl.when((z >= slot) & (z < n_chip - 1))(
                    lambda: z_copy(k, slot, t, 0).wait_send()
                )
                pl.when((z <= slot) & (z > 0))(lambda: z_copy(k, slot, t, 1).wait_send())

    def g_copy(k, slot, target):
        return remote(gr.at[k, slot], gr.at[k, slot], g_send.at[k, target], g_recv.at[k, slot], (target, w))

    def p_copy(k, slot, target):
        return remote(ps.at[k, target], pr.at[k, slot], p_send.at[k, target], p_recv.at[k, slot], (target, w))

    def q_copy(k, dest, t, way):
        target = z + 1 - 2 * way
        return remote(
            qs.at[k, dest, t], qr.at[k, way, dest, t], q_send.at[k, dest, t], q_recv.at[k, way, dest, t],
            (l, 2 * target + c),
        )

    def q_add(k, dest, way):
        for t in range(2):
            q_copy(k, dest, t, way).wait_recv()
            total = qs[k, dest, t].astype(jnp.float32) + qr[k, way, dest, t].astype(jnp.float32)
            qs[k, dest, t] = total.astype(jnp.bfloat16)
            q_copy(k, dest, t, way).start()

    def q_stage(k, j):
        up, down = n_chip - 1 - j, j
        upper = z >= n_chip // 2
        goes_down = (z < n_chip - 1) & (z > down)
        pl.when(goes_down & upper)(lambda: q_add(k, down, 1))
        pl.when((z > 0) & (z < up))(lambda: q_add(k, up, 0))
        pl.when(goes_down & (z < n_chip // 2))(lambda: q_add(k, down, 1))

    cot_x = remote(cot_ref.at[oc], gr.at[0, l, c], ex_send.at[1], ex_recv.at[1], partner)
    cot_x.start()
    tele_x = remote(tele_ref.at[oc], zc.at[0, z, c], ex_send.at[0], ex_recv.at[0], partner)
    tele_x.start()
    gr[0, l, c] = cot_ref[c]
    zc[0, z, c] = tele_ref[c]
    cot_x.wait()
    for lp in loop_peers:
        g_copy(0, l, lp).start()
    tele_x.wait()
    z_pass(0, z, 0)
    load.wait()

    def forward_part(k, lp):
        total = None
        for zp in range(n_chip):
            part = jnp.dot(
                tiles[lp, zp].reshape(2 * items, 2 * items),
                zc[k, zp].reshape(2 * items, half),
                preferred_element_type=jnp.float32,
            )
            total = part if total is None else total + part
        return total

    def adjoint_part(k, zp):
        total = None
        for lp in range(n_loop):
            for t in range(2):
                part = jnp.dot(gr[k, lp, t], tiles[lp, zp, t], preferred_element_type=jnp.float32)
                total = part if total is None else total + part
        return total

    for k in range(STEPS):
        if n_chip > 1:
            z_pass(k, z, 1)
        for lp in loop_peers:
            g_copy(k, lp, l).wait_recv()

        def q_step(j, carry):
            flip = (2 * z) // n_chip
            zp = (1 - flip) * (n_chip - 1 - j) + flip * j

            @pl.when(zp != z)
            def _():
                value = adjoint_part(k, zp).astype(jnp.bfloat16)
                for t in range(2):
                    qs[k, zp, t] = value[:, t * items : (t + 1) * items]
                for t in range(2):
                    pl.when(z == 0)(lambda: q_copy(k, zp, t, 0).start())
                    pl.when(z == n_chip - 1)(lambda: q_copy(k, zp, t, 1).start())

            return carry

        lax.fori_loop(0, n_chip, q_step, 0)
        own_q[...] = adjoint_part(k, z)
        for held in range(2, n_chip - 1):
            z_pass(k, z, held)
        q_stage(k, 0)
        if n_chip > 2:
            z_pass(k, z, n_chip - 1)

        def p_step(j, carry):
            lp = lax.rem(l + 1 + j, n_loop)
            ps[k, lp] = forward_part(k, lp).astype(jnp.bfloat16)
            p_copy(k, l, lp).start()
            return carry

        lax.fori_loop(0, n_loop - 1, p_step, 0)
        own_p = forward_part(k, l)

        for j in range(1, n_chip - 1):
            q_stage(k, j)
        for t in range(2):
            lanes = slice(t * items, (t + 1) * items)
            for way, inside in ((0, z > 0), (1, z < n_chip - 1)):

                @pl.when(inside)
                def _():
                    q_copy(k, z, t, way).wait_recv()
                    own_q[:, lanes] = own_q[:, lanes] + qr[k, way, z, t].astype(jnp.float32)

            gr[k + 1, l, t] = ((1.0 - ALPHA) * own_q[:, lanes]).astype(jnp.bfloat16)
        if k < STEPS - 1:
            for lp in loop_peers:
                g_copy(k + 1, l, lp).start()
        else:
            for t in range(2):
                kept = gr[0, l, t].astype(jnp.float32)
                for step in range(1, STEPS):
                    kept = kept + gr[step, l, t].astype(jnp.float32)
                gt_s[t] = (ALPHA * kept + gr[STEPS, l, t].astype(jnp.float32)).astype(jnp.bfloat16)
            gt_copy = remote(gt_s.at[oc], gt.at[c], ex_send.at[3], ex_recv.at[3], partner)
            gt_copy.start()
            gt[c] = gt_s[c]

        for lp in loop_peers:
            p_copy(k, lp, l).wait_recv()
        total = own_p
        for lp in loop_peers:
            total = total + pr[k, lp].astype(jnp.float32)
        teleport = zc[0, z].reshape(2 * items, half).astype(jnp.float32)
        mixed = ((1.0 - ALPHA) * total + ALPHA * teleport).astype(jnp.bfloat16)
        if k < STEPS - 1:
            for t in range(2):
                zc[k + 1, z, t] = mixed[t * items : (t + 1) * items]
            z_pass(k + 1, z, 0)
        else:
            for t in range(2):
                prop_s[t] = mixed[t * items : (t + 1) * items]
            prop_copy = remote(prop_s.at[oc], prop_x, ex_send.at[2], ex_recv.at[2], partner)
            prop_copy.start()

    gt_copy.wait()
    grad_teleport = gt[...].reshape(2 * half, items)
    contract_last = (((1,), (1,)), ((), ()))
    second_sum = lax.dot_general(
        hidden_ref[...], grad_teleport, contract_last, preferred_element_type=jnp.float32
    )
    rows_f, cols_f = f_s.shape[3], f_s.shape[4]
    rows_s = s_s.shape[3]
    for cc in range(2):
        for lp in range(n_loop):
            for zp in range(n_chip):
                row = ((2 * zp + cc) * n_loop + lp) * rows_s
                s_s[cc, lp, zp] = second_sum[row : row + rows_s].astype(jnp.bfloat16)

    def pair_copy(which, src, dst):
        return remote(src.at[oc], dst, pair_send.at[which], pair_recv.at[which], partner)

    def lane_copy(which, src, dst, slot, target):
        return remote(src.at[target], dst.at[slot], lane_send.at[which, target], lane_recv.at[which, slot], (target, w))

    def chip_copy(which, src, dst, slot, target):
        return remote(
            src.at[target], dst.at[slot], chip_send.at[which, target], chip_recv.at[which, slot],
            (l, 2 * target + c),
        )

    def last_copy(which, ref, slot, target):
        return remote(ref.at[slot], ref.at[slot], last_send.at[which, target], last_recv.at[which, slot], (target, w))

    pair_copy(1, s_s, s_x).start()
    grad_hidden = jnp.dot(second_ref[...], grad_teleport, preferred_element_type=jnp.float32)
    grad_pre = (grad_hidden * slope_ref[...]).astype(jnp.bfloat16)
    first_sum = lax.dot_general(
        feats_ref[...], grad_pre, contract_last, preferred_element_type=jnp.float32
    )
    for cc in range(2):
        for lp in range(n_loop):
            for zp in range(n_chip):
                row = (2 * zp + cc) * rows_f
                f_s[cc, lp, zp] = first_sum[
                    row : row + rows_f, lp * cols_f : (lp + 1) * cols_f
                ].astype(jnp.bfloat16)
    pair_copy(0, f_s, f_x).start()
    sets = (
        (1, s_s, s_x, s_h, s_p, s_q, s_r, s_g),
        (0, f_s, f_x, f_h, f_p, f_q, f_r, f_g),
    )
    wide = jnp.float32
    for which, own, got, sums, _p, _q, _r, _g in sets:
        pair_copy(which, own, got).wait()
        for lp in loop_peers:
            sums[lp] = (own[c, lp].astype(wide) + got[lp].astype(wide)).astype(jnp.bfloat16)
            lane_copy(which, sums, _p, l, lp).start()
    for which, own, got, sums, parts, quarter, _r, _g in sets:
        total = own[c, l].astype(wide) + got[l].astype(wide)
        for lp in loop_peers:
            lane_copy(which, sums, parts, lp, l).wait_recv()
            total = total + parts[lp].astype(wide)
        quarter[...] = total.astype(jnp.bfloat16)
        for zp in chip_peers:
            chip_copy(which, quarter, _r, z, zp).start()
    for which, _o, _x, _h, _p, quarter, pieces, final in sets:
        total = quarter[z].astype(wide)
        for zp in chip_peers:
            chip_copy(which, quarter, pieces, zp, z).wait_recv()
            total = total + pieces[zp].astype(wide)
        final[l] = total.astype(jnp.bfloat16)
        for lp in loop_peers:
            last_copy(which, final, l, lp).start()
    prop_copy.wait()
    for side in range(2):

        @pl.when(c == side)
        def _():
            prop_ref[:, side * half : (side + 1) * half] = prop_s[side]
            prop_ref[:, (1 - side) * half : (2 - side) * half] = prop_x[...]

    for k in range(STEPS):
        z_sent(k)
        for t in range(2):
            for dest in range(n_chip):
                pl.when(z < dest)(lambda: q_copy(k, dest, t, 0).wait_send())
                pl.when(z > dest)(lambda: q_copy(k, dest, t, 1).wait_send())
        for lp in loop_peers:
            g_copy(k, l, lp).wait_send()
            p_copy(k, l, lp).wait_send()
    for which, _o, _x, sums, parts, quarter, pieces, final in sets:
        for lp in loop_peers:
            lane_copy(which, sums, parts, l, lp).wait_send()
            last_copy(which, final, l, lp).wait_send()
        for zp in chip_peers:
            chip_copy(which, quarter, pieces, z, zp).wait_send()
        for lp in loop_peers:
            last_copy(which, final, lp, l).wait_recv()
    for lp in range(n_loop):
        first_out[:, lp * cols_f : (lp + 1) * cols_f] = f_g[lp]
        second_out[lp * rows_s : (lp + 1) * rows_s, :] = s_g[lp]


def sum_buffers(n_loop, n_chip, rows, cols):
    shapes = (
        (2, n_loop, n_chip, rows, cols),
        (n_loop, n_chip, rows, cols),
        (n_loop, n_chip, rows, cols),
        (n_loop, n_chip, rows, cols),
        (n_chip, rows, cols),
        (n_chip, rows, cols),
        (n_loop, rows, cols),
    )
    return [pltpu.VMEM(shape, jnp.bfloat16) for shape in shapes]


def power_steps(tele, cot, feats, hidden, slope, second, dense, n_loop, n_chip):
    _, items, half = tele.shape
    features, units = feats.shape[0], hidden.shape[0]
    first_rows, second_rows = features // (2 * n_chip), units // (2 * n_chip)
    bf16, dma = jnp.bfloat16, pltpu.SemaphoreType.DMA
    vmem = pl.BlockSpec(memory_space=pltpu.VMEM)
    return pl.pallas_call(
        functools.partial(power_kernel, n_loop, n_chip),
        out_shape=(
            jax.ShapeDtypeStruct((items, 2 * half), bf16),
            jax.ShapeDtypeStruct((first_rows, units), bf16),
            jax.ShapeDtypeStruct((second_rows, features), bf16),
        ),
        in_specs=[vmem] * 6 + [pl.BlockSpec(memory_space=pl.ANY)],
        out_specs=(vmem, vmem, vmem),
        scratch_shapes=[
            pltpu.VMEM(dense.shape, bf16),
            pltpu.VMEM((STEPS, n_chip, 2, items, half), bf16),
            pltpu.VMEM((STEPS + 1, n_loop, 2, half, items), bf16),
            pltpu.VMEM((STEPS, n_loop, 2 * items, half), bf16),
            pltpu.VMEM((STEPS, n_loop, 2 * items, half), bf16),
            pltpu.VMEM((STEPS, n_chip, 2, half, items), bf16),
            pltpu.VMEM((STEPS, 2, n_chip, 2, half, items), bf16),
            pltpu.VMEM((half, 2 * items), jnp.float32),
            pltpu.VMEM((items, half), bf16),
            pltpu.VMEM((2, half, items), bf16),
            pltpu.VMEM((2, items, half), bf16),
            pltpu.VMEM((2, half, items), bf16),
            *sum_buffers(n_loop, n_chip, first_rows, units // n_loop),
            *sum_buffers(n_loop, n_chip, second_rows // n_loop, features),
            dma,
            dma((4,)),
            dma((4,)),
            dma((STEPS, 2, n_chip, 2)),
            dma((STEPS, n_chip, 2)),
            dma((STEPS, n_loop)),
            dma((STEPS, n_loop)),
            dma((STEPS, n_loop)),
            dma((STEPS, n_loop)),
            dma((STEPS, n_chip, 2)),
            dma((STEPS, 2, n_chip, 2)),
            dma((2,)),
            dma((2,)),
            dma((2, n_loop)),
            dma((2, n_loop)),
            dma((2, n_chip)),
            dma((2, n_chip)),
            dma((2, n_loop)),
            dma((2, n_loop)),
        ],
        compiler_params=pltpu.CompilerParams(
            collective_id=0, has_side_effects=True, vmem_limit_bytes=63 * 2**20
        ),
        name="power_steps",
    )(tele, cot, feats, hidden, slope, second, dense)


def body(feats, w_first, w_second, cotangent, block_values, row_ptr, col_idx):
    n_loop, n_wide = lax.axis_size("loop"), lax.axis_size("wide")
    n_chip = n_wide // 2
    mine = block_values[0, 0]
    index = jnp.concatenate([row_ptr[0, 0], col_idx[0, 0]])
    swap = [(i, i + 1 - 2 * (i % 2)) for i in range(n_wide)]
    other = lax.ppermute(mine, "wide", swap)
    other_index = lax.ppermute(index, "wide", swap)
    flat_feats = feats[0]
    items, features = flat_feats.shape
    half = features // 2
    pre_act = lax.dot_general(
        w_first, flat_feats, (((0,), (1,)), ((), ())), preferred_element_type=jnp.float32
    )
    hidden = jax.nn.silu(pre_act).astype(jnp.bfloat16)
    teleport = lax.dot_general(
        hidden, w_second, (((0,), (0,)), ((), ())), preferred_element_type=jnp.float32
    ).astype(jnp.bfloat16)
    core = lax.rem(lax.axis_index("wide"), 2).astype(jnp.int32).reshape(1)
    dense = dense_pair(
        jnp.stack([index, other_index]), core, mine, other, n_loop, n_chip, items
    )
    current, grad_first, grad_second = power_steps(
        teleport.reshape(items, 2, half).transpose(1, 0, 2),
        cotangent[0].T.reshape(2, half, items),
        flat_feats.T,
        hidden,
        silu_slope(pre_act),
        w_second,
        dense,
        n_loop,
        n_chip,
    )
    return (current[None], grad_first.astype(jnp.float32), grad_second.astype(jnp.float32))


def solution(mesh):
    return jax.shard_map(
        body,
        mesh=mesh,
        in_specs=(
            P("wide", "loop", None),
            P(),
            P(),
            P("wide", "loop", None),
            P("loop", "wide", None, None, None),
            P("loop", "wide", None),
            P("loop", "wide", None),
        ),
        out_specs=(P("wide", "loop", None), P("wide", None), P("wide", None)),
        check_vma=False,
    )
```
